32 devices in a mesh: groups: 2 (over x), patch: 16 (over z, y, core).
Axes of the slice: x: 2, y: 2, z: 4, core: 2. Of those that a mesh axis runs over, the one named last changes fastest.
Arguments:
- points: bfloat16 [32768, 512], P(('groups', 'patch')), parts along dimension 0, may hold values from -6 to 6
- lengths: int32 [32], P(('groups', 'patch')), parts along dimension 0, may hold values from 1 to 1024, 12288 in all
- send_blocks: int32 [32, 2, 3], P(('groups', 'patch')), parts along dimension 0, may hold values from 0 to 7, as said below
- pattern: int32 [256, 3], P(('groups', 'patch')), parts along dimension 0, may hold values from 0 to 13, as said below
- ln1_gain: float32 [512], replicated, may hold values from 0.25 to 1.75
- qk_weight: bfloat16 [2, 512, 512], replicated
- v_weight: bfloat16 [512, 512], replicated, may hold values from -0.25 to 0.25
- o_weight: bfloat16 [512, 512], replicated, may hold values from -0.25 to 0.25
- ln2_gain: float32 [512], replicated, may hold values from 0.25 to 1.75
- up_weight: bfloat16 [512, 2048], replicated, may hold values from -0.25 to 0.25
- down_weight: bfloat16 [2048, 512], replicated, may hold values from -0.125 to 0.125
Outputs:
- block_out: bfloat16 [32768, 512], P(('groups', 'patch')), parts along dimension 0
The draws below stay inside these ranges and needn't reach their ends.
There are 2 independent parts, one for each index of `groups`. The reference program is written for one: setup_inputs(seed, part) draws one part's arguments, and reference() takes and returns one part's arrays. A program takes and returns all parts, laid end to end along the dimension named above; an argument that names none is the same for every part. Nothing has to cross between parts.
Inputs may be any that keep to these rules, and one draw needn't show every extreme that they name: `send_blocks`: for each patch the 6 entries are distinct local blocks; [p, 0, :] are offered to patch p - 1 and [p, 1, :] to patch p + 1. `pattern`: row r belongs to block r % 8 of patch r // 8; its entries are distinct slots other than r % 8; the first patch names no slot from 8 to 10, the last patch no slot from 11 on. `lengths`: they sum to 12288; some patch is full.
All inputs are finite; a program needn't handle non-finite values. No bound on the sum of `lengths` on one device may be relied on, other than what follows from the above.
Results may differ from the reference program's by a relative error of at most 0.011.
Values may be sent and summed in bfloat16 or wider, within the bound.
A program may use at most 64 MiB of HBM per device.

```python
import math
import jax
import jax.numpy as jnp
import numpy as np
from jax import lax

D = 512
H = 32
FF = 2048
BLK = 128
NEIGH = 3
SEND = 3
BLK_DEV = 8
HD = 16
P_DEV = 1024
BLOCKS = 128
ROWS = 16384
N_PATCH = 16


def draw_send_blocks(key, part):
    dev_count = BLOCKS // BLK_DEV
    scores = jax.random.randint(key, (dev_count, BLK_DEV), 0, 2 ** 20) * BLK_DEV + jnp.arange(BLK_DEV, dtype=jnp.int32)[None, :]
    order = jnp.argsort(scores, axis=1, stable=True).astype(jnp.int32)
    return order[:, :2 * SEND].reshape(dev_count, 2, SEND)


def draw_pattern(key, part):
    dev_count = BLOCKS // BLK_DEV
    slot_count = BLK_DEV + 2 * SEND
    row_ids = jnp.arange(BLOCKS, dtype=jnp.int32)[:, None]
    device = row_ids // BLK_DEV
    local = row_ids % BLK_DEV
    column = jnp.arange(slot_count, dtype=jnp.int32)[None, :]
    scores = jax.random.randint(key, (BLOCKS, slot_count), 0, 2 ** 20) * slot_count + column
    invalid = (column == local) | (device == 0) & (column >= BLK_DEV) & (column < BLK_DEV + SEND) | (device == dev_count - 1) & (column >= BLK_DEV + SEND)
    forced = (local < 2 * SEND) & (column == BLK_DEV + local) & jnp.logical_not(invalid)
    scores = jnp.where(forced, 2 ** 30, jnp.where(invalid, -1, scores))
    unused, picked = lax.top_k(scores, NEIGH)
    return picked.astype(jnp.int32)


def draw_qk_weight(key, part):
    first, second = jax.random.split(key, 2)
    key_side = jax.random.normal(first, (D, D), jnp.float32) / math.sqrt(D)
    noise = jax.random.normal(second, (D, D), jnp.float32) / math.sqrt(D)
    query_side = noise
    return jnp.stack([query_side, key_side]).astype(jnp.bfloat16)


def level_of(key, shape, cuts, smallest, high):
    factor_of = 1.0
    for dim, parts in cuts:
        steps = jax.random.uniform(jax.random.fold_in(jax.random.fold_in(key, 6), dim), (parts,), jnp.float32, smallest / len(cuts), high / len(cuts))
        factor_of = factor_of * jnp.repeat(jnp.exp(steps), shape[dim] // parts).reshape((-1,) + (1,) * (len(shape) - 1 - dim))
    return factor_of


def split_up(count, total, reach, lean):
    loads = [(1 << 20) // math.isqrt(grade ** lean) + 1 for grade in range(2, count + 1)]
    surplus, holding = total - reach - (count - 1), [1] * (count - 1)
    while surplus > 0:
        candidates = [i for i in range(count - 1) if holding[i] < reach]
        mass, left = sum([loads[i] for i in candidates]), surplus
        for i in candidates:
            addition = min(reach - holding[i], max(1, left * loads[i] // mass), surplus)
            holding[i] = holding[i] + addition
            surplus = surplus - addition
    return np.array([reach] + holding)


def uneven(own_key, amount, total, limit, skew):
    if amount == 2:
        one = jax.random.randint(own_key, (), max(1, total - limit), min(limit, total - 1) + 1)
        return jnp.stack([one, total - one])
    sizes = jnp.asarray(split_up(amount, total, limit, skew), jnp.int32)
    pairs = (amount - 1) // 2
    donor, sink = sizes[1:1 + 2 * pairs:2], sizes[2:2 + 2 * pairs:2]
    margin = jnp.minimum(donor - 1, limit - sink)
    moved = jax.random.randint(jax.random.fold_in(own_key, 1), (pairs,), 0, 1 << 20) % (margin + 1)
    sizes = sizes.at[1:1 + 2 * pairs:2].set(donor - moved).at[2:2 + 2 * pairs:2].set(sink + moved)
    return sizes[jax.random.permutation(jax.random.fold_in(own_key, 2), amount)]


def centred(stream_key, dims, scale, most, cuts=(), kind=jnp.bfloat16):
    drawn = jax.random.normal(stream_key, dims, jnp.float32) * scale
    if len(cuts) > 0:
        drawn = level_of(stream_key, dims, cuts, -0.22, 0.18) * drawn
    return jnp.clip(drawn, min=-most, max=most).astype(kind)


def setup_inputs(seed: int = 0, part: int = 0) -> dict:
    keys = jax.random.split(jax.random.key(seed), 12)
    part_splits = jax.random.split(jax.random.fold_in(keys[11], part), 12)
    return {
        "points": centred(part_splits[0], (ROWS, D), 1.0, 6.0, ((0, 16),)),
        "lengths": uneven(part_splits[1], N_PATCH, N_PATCH * P_DEV * 3 // 4, P_DEV, 1).astype(jnp.int32),
        "send_blocks": draw_send_blocks(jax.random.fold_in(jax.random.fold_in(keys[11], part), 71), part),
        "pattern": draw_pattern(jax.random.fold_in(jax.random.fold_in(keys[11], part), 71), part),
        "ln1_gain": jnp.clip(1.0 + 0.15 * jax.random.normal(keys[4], (D,), jnp.float32), 0.25, 1.75),
        "qk_weight": draw_qk_weight(jax.random.fold_in(keys[11], 71), part),
        "v_weight": centred(keys[6], (D, D), D ** -0.5, 0.25),
        "o_weight": centred(keys[7], (D, D), D ** -0.5, 0.25),
        "ln2_gain": jnp.clip(1.0 + 0.15 * jax.random.normal(keys[8], (D,), jnp.float32), 0.25, 1.75),
        "up_weight": centred(keys[9], (D, FF), D ** -0.5, 0.25),
        "down_weight": centred(keys[10], (FF, D), FF ** -0.5, 0.125),
    }


def layer_norm(inputs, gain):
    center = inputs - lax.optimization_barrier(jnp.mean(inputs, axis=-1, keepdims=True))
    spread = lax.optimization_barrier(jnp.mean(center * center, axis=-1, keepdims=True))
    return center * lax.rsqrt(spread + 1e-05) * gain

def attend_blocks(queries, pool_keys, pool_values, pool_bias, picks):
    scale = 1.0 / math.sqrt(HD)

    def one_block(index):
        chosen = jnp.concatenate([index[None].astype(jnp.int32), picks[index].astype(jnp.int32)])
        key_rows = jnp.take(pool_keys, chosen, axis=0).reshape(-1, H, HD)
        value_rows = jnp.take(pool_values, chosen, axis=0).reshape(-1, H, HD)
        bias_rows = jnp.take(pool_bias, chosen, axis=0).reshape(-1).astype(jnp.float32)
        scores = jnp.einsum('qhd,khd->hqk', queries[index].astype(jnp.float32), key_rows.astype(jnp.float32)) * scale
        scores = scores + bias_rows[None, None, :]
        top = lax.optimization_barrier(jnp.max(scores, axis=-1, keepdims=True))
        expo = jnp.exp(scores - top)
        weights = (expo / lax.optimization_barrier(jnp.sum(expo, axis=-1, keepdims=True))).astype(jnp.bfloat16)
        mixed = jnp.einsum('hqk,khd->qhd', weights.astype(jnp.float32), value_rows.astype(jnp.float32))
        return mixed.astype(jnp.bfloat16)
    return lax.map(one_block, jnp.arange(queries.shape[0], dtype=jnp.int32))

def reference(points, lengths, send_blocks, pattern, ln1_gain, qk_weight, v_weight, o_weight, ln2_gain, up_weight, down_weight):
    dev_count = BLOCKS // BLK_DEV
    inputs = points.astype(jnp.float32)
    normed = layer_norm(inputs, ln1_gain).astype(jnp.bfloat16)
    queries = jnp.dot(normed, qk_weight[0], preferred_element_type=jnp.float32).astype(jnp.bfloat16)
    keys_all = jnp.dot(normed, qk_weight[1], preferred_element_type=jnp.float32).astype(jnp.bfloat16)
    values_all = jnp.dot(normed, v_weight, preferred_element_type=jnp.float32).astype(jnp.bfloat16)
    position = jnp.arange(P_DEV, dtype=jnp.int32)
    valid = position[None, :] < lengths[:, None]
    key_bias = jnp.where(valid, 0.0, -1000000000.0).astype(jnp.bfloat16)
    device_ids = jnp.arange(dev_count, dtype=jnp.int32)[:, None]

    def build_pool(blocks):
        to_right = blocks[device_ids, send_blocks[:, 1, :]]
        to_left = blocks[device_ids, send_blocks[:, 0, :]]
        from_left = jnp.concatenate([jnp.zeros_like(to_right[:1]), to_right[:-1]], axis=0)
        from_right = jnp.concatenate([to_left[1:], jnp.zeros_like(to_left[:1])], axis=0)
        return jnp.concatenate([blocks, from_left, from_right], axis=1)
    pool_keys = build_pool(keys_all.reshape(dev_count, BLK_DEV, BLK, D))
    pool_values = build_pool(values_all.reshape(dev_count, BLK_DEV, BLK, D))
    pool_bias = build_pool(key_bias.reshape(dev_count, BLK_DEV, BLK))
    query_blocks = queries.reshape(dev_count, BLK_DEV, BLK, H, HD)
    picks = pattern.reshape(dev_count, BLK_DEV, NEIGH)

    def per_device(packed):
        return attend_blocks(packed[0], packed[1], packed[2], packed[3], packed[4])
    attended = lax.map(per_device, (query_blocks, pool_keys, pool_values, pool_bias, picks)).reshape(ROWS, D)
    mixed = inputs + jnp.dot(attended, o_weight, preferred_element_type=jnp.float32)
    normed_two = layer_norm(mixed, ln2_gain).astype(jnp.bfloat16)
    hidden = jax.nn.gelu(jnp.dot(normed_two, up_weight, preferred_element_type=jnp.float32), approximate=False).astype(jnp.bfloat16)
    result = mixed + jnp.dot(hidden, down_weight, preferred_element_type=jnp.float32)
    return jnp.where(valid.reshape(-1)[:, None], result, 0.0).astype(jnp.bfloat16)
```

```python
import functools
import math

import jax
import jax.numpy as jnp
from jax import lax
from jax.experimental import pallas as pl
from jax.experimental.pallas import tpu as pltpu
from jax.sharding import PartitionSpec as P

H = 32
LANES = 128
MARK = 1000.0
NEG = -1000000000.0
LOG2E = 1.4426950408889634
STACK = 4


def passed_along(array, axis, by):
    count = lax.axis_size(axis)
    pairs = [(i, i + by) for i in range(count) if 0 <= i + by < count]
    return lax.ppermute(array, axis, pairs)


def layer_norm(inputs, gain):
    center = inputs - jnp.mean(inputs, axis=-1, keepdims=True)
    spread = jnp.mean(center * center, axis=-1, keepdims=True)
    return center * lax.rsqrt(spread + 1e-05) * gain


def pack_kernel(send_ref, length_ref, first_ref, second_ref, right_ref, left_ref):
    step = pl.program_id(0)
    rows = first_ref.shape[0]
    for block, source, target in (
        (send_ref[1, step], first_ref, right_ref),
        (send_ref[0, step], second_ref, left_ref),
    ):
        position = block * rows + lax.broadcasted_iota(jnp.int32, source.shape, 0)
        value = source[...].astype(jnp.float32)
        target[...] = jnp.where(position < length_ref[0], value, MARK).astype(target.dtype)


def pack(points, send, lengths, block_rows):
    width = points.shape[1]
    count = send.shape[1]
    shape = jax.ShapeDtypeStruct((count * block_rows, width), points.dtype)
    return pl.pallas_call(
        pack_kernel,
        out_shape=(shape, shape),
        grid_spec=pltpu.PrefetchScalarGridSpec(
            num_scalar_prefetch=2,
            grid=(count,),
            in_specs=[
                pl.BlockSpec((block_rows, width), lambda s, send, _: (send[1, s], 0)),
                pl.BlockSpec((block_rows, width), lambda s, send, _: (send[0, s], 0)),
            ],
            out_specs=[
                pl.BlockSpec((block_rows, width), lambda s, send, _: (s, 0)),
                pl.BlockSpec((block_rows, width), lambda s, send, _: (s, 0)),
            ],
        ),
        name="pack",
    )(send, lengths, points, points)


def project_kernel(scale, x_ref, gain_ref, qk_ref, v_ref, q_out, k_out, v_out):
    normed = layer_norm(x_ref[...].astype(jnp.float32), gain_ref[...]).astype(jnp.bfloat16)
    queries = jnp.dot(normed, qk_ref[0], preferred_element_type=jnp.float32)
    q_out[...] = (queries * scale).astype(q_out.dtype)
    k_out[...] = jnp.dot(normed, qk_ref[1], preferred_element_type=jnp.float32).astype(k_out.dtype)
    v_out[...] = jnp.dot(normed, v_ref[...], preferred_element_type=jnp.float32).astype(v_out.dtype)


def project(points, gain, qk_weight, v_weight, scale, tile=256):
    rows, width = points.shape
    shape = jax.ShapeDtypeStruct((rows, width), jnp.bfloat16)
    row_spec = pl.BlockSpec((tile, width), lambda i: (i, 0))
    return pl.pallas_call(
        functools.partial(project_kernel, scale),
        out_shape=(shape, shape, shape),
        grid=(rows // tile,),
        in_specs=[
            row_spec,
            pl.BlockSpec(gain.shape, lambda i: (0, 0)),
            pl.BlockSpec(qk_weight.shape, lambda i: (0, 0, 0)),
            pl.BlockSpec(v_weight.shape, lambda i: (0, 0)),
        ],
        out_specs=[row_spec] * 3,
        cost_estimate=pl.CostEstimate(
            flops=6 * rows * width * width,
            bytes_accessed=8 * rows * width + 6 * width * width,
            transcendentals=0,
        ),
        name="project",
    )(points, gain, qk_weight, v_weight)


def attend_kernel(
    block_rows,
    head_size,
    pattern_ref,
    length_ref,
    q_ref,
    k_ref,
    v_ref,
    left_ref,
    right_ref,
    gain_ref,
    wk_ref,
    wv_ref,
    out_ref,
    k_pool,
    v_pool,
    b_pool,
):
    step = pl.program_id(0)
    local, width = k_ref.shape
    offered = left_ref.shape[0]
    per_tile = LANES // head_size
    first_lane = lambda shape: lax.broadcasted_iota(jnp.int32, shape, 1) == 0

    @pl.when(step == 0)
    def _():
        k_pool[0:local, :] = k_ref[...]
        v_pool[0:local, :] = v_ref[...]
        position = lax.broadcasted_iota(jnp.int32, (local, LANES), 0)
        dead = (position >= length_ref[0]) & first_lane((local, LANES))
        b_pool[0:local, :] = jnp.where(dead, NEG, 0.0).astype(b_pool.dtype)
        for index, source in enumerate((left_ref, right_ref)):
            start = local + index * offered
            rows = source[...].astype(jnp.float32)
            normed = layer_norm(rows, gain_ref[...]).astype(jnp.bfloat16)
            k_pool[start : start + offered, :] = jnp.dot(
                normed, wk_ref[0], preferred_element_type=jnp.float32
            ).astype(k_pool.dtype)
            v_pool[start : start + offered, :] = jnp.dot(
                normed, wv_ref[...], preferred_element_type=jnp.float32
            ).astype(v_pool.dtype)
            dead = (rows[:, 0:LANES] > 0.5 * MARK) & first_lane((offered, LANES))
            b_pool[start : start + offered, :] = jnp.where(dead, NEG, 0.0).astype(b_pool.dtype)

    slots = [step] + [pattern_ref[step, s] for s in range(pattern_ref.shape[1])]
    starts = [pl.multiple_of(slot * block_rows, block_rows) for slot in slots]
    lane = lax.broadcasted_iota(jnp.int32, (block_rows, LANES), 1)
    unit = jnp.where(lane == 0, 1.0, 0.0).astype(jnp.bfloat16)
    bias = jnp.concatenate([b_pool[pl.ds(start, block_rows), :] for start in starts], axis=0)
    ones = jnp.ones((len(slots) * block_rows, LANES), jnp.bfloat16)

    for tile in range(width // LANES):
        columns = pl.ds(tile * LANES, LANES)
        keys = jnp.concatenate(
            [k_pool[pl.ds(start, block_rows), columns] for start in starts], axis=0
        )
        values = jnp.concatenate(
            [v_pool[pl.ds(start, block_rows), columns] for start in starts], axis=0
        )
        keys = jnp.concatenate([keys, bias], axis=1)
        values = jnp.concatenate([values, ones], axis=1)
        queries = q_ref[:, columns].astype(jnp.float32)
        top = bottom = None
        for group in range(0, per_tile, STACK):
            heads = range(group, group + STACK)
            stacked = jnp.concatenate(
                [
                    jnp.concatenate(
                        [
                            jnp.where(lane // head_size == head, queries, 0.0).astype(jnp.bfloat16),
                            unit,
                        ],
                        axis=1,
                    )
                    for head in heads
                ],
                axis=0,
            )
            scores = lax.dot_general(
                stacked, keys, (((1,), (1,)), ((), ())), preferred_element_type=jnp.float32
            )
            expo = jnp.exp2(scores - jnp.max(scores, axis=-1, keepdims=True)).astype(jnp.bfloat16)
            mixed = jnp.dot(expo, values, preferred_element_type=jnp.float32)
            for index, head in enumerate(heads):
                part = mixed[index * block_rows : (index + 1) * block_rows]
                num, den = part[:, :LANES], part[:, LANES:]
                if top is None:
                    top, bottom = num, den
                else:
                    mine = lane // head_size == head
                    top = jnp.where(mine, num, top)
                    bottom = jnp.where(mine, den, bottom)
        out_ref[:, columns] = (top / bottom).astype(out_ref.dtype)


def attend(queries, keys, values, left, right, pattern, lengths, gain, qk_weight, v_weight):
    rows, width = queries.shape
    blocks = pattern.shape[0]
    block_rows = rows // blocks
    pool = rows + left.shape[0] + right.shape[0]
    row_spec = pl.BlockSpec((block_rows, width), lambda i, *_: (i, 0))
    whole = lambda shape: pl.BlockSpec(shape, lambda i, *_: (0,) * len(shape))
    return pl.pallas_call(
        functools.partial(attend_kernel, block_rows, width // H),
        out_shape=jax.ShapeDtypeStruct((rows, width), jnp.bfloat16),
        grid_spec=pltpu.PrefetchScalarGridSpec(
            num_scalar_prefetch=2,
            grid=(blocks,),
            in_specs=[
                row_spec,
                whole(keys.shape),
                whole(values.shape),
                whole(left.shape),
                whole(right.shape),
                whole(gain.shape),
                pl.BlockSpec((1, width, width), lambda i, *_: (1, 0, 0)),
                whole(v_weight.shape),
            ],
            out_specs=row_spec,
            scratch_shapes=[
                pltpu.VMEM((pool, width), jnp.bfloat16),
                pltpu.VMEM((pool, width), jnp.bfloat16),
                pltpu.VMEM((pool, LANES), jnp.bfloat16),
            ],
        ),
        compiler_params=pltpu.CompilerParams(vmem_limit_bytes=48 << 20),
        name="attend",
    )(pattern, lengths, queries, keys, values, left, right, gain, qk_weight, v_weight)


def mix_kernel(length_ref, x_ref, a_ref, wo_ref, gain_ref, up_ref, down_ref, out_ref):
    rows = x_ref.shape[0]
    mixed = x_ref[...].astype(jnp.float32) + jnp.dot(
        a_ref[...], wo_ref[...], preferred_element_type=jnp.float32
    )
    normed = layer_norm(mixed, gain_ref[...]).astype(jnp.bfloat16)
    inner = jnp.dot(normed, up_ref[...], preferred_element_type=jnp.float32)
    hidden = (0.5 * inner * (1.0 + lax.erf(inner * math.sqrt(0.5)))).astype(jnp.bfloat16)
    result = mixed + jnp.dot(hidden, down_ref[...], preferred_element_type=jnp.float32)
    position = pl.program_id(0) * rows + lax.broadcasted_iota(jnp.int32, result.shape, 0)
    out_ref[...] = jnp.where(position < length_ref[0], result, 0.0).astype(out_ref.dtype)


def mix(points, attended, lengths, o_weight, gain, up_weight, down_weight, tile=256):
    rows, width = points.shape
    row_spec = pl.BlockSpec((tile, width), lambda i, *_: (i, 0))
    whole = lambda shape: pl.BlockSpec(shape, lambda i, *_: (0,) * len(shape))
    return pl.pallas_call(
        mix_kernel,
        out_shape=jax.ShapeDtypeStruct((rows, width), jnp.bfloat16),
        grid_spec=pltpu.PrefetchScalarGridSpec(
            num_scalar_prefetch=1,
            grid=(rows // tile,),
            in_specs=[
                row_spec,
                row_spec,
                whole(o_weight.shape),
                whole(gain.shape),
                whole(up_weight.shape),
                whole(down_weight.shape),
            ],
            out_specs=row_spec,
        ),
        compiler_params=pltpu.CompilerParams(vmem_limit_bytes=48 << 20),
        name="mix",
    )(lengths, points, attended, o_weight, gain, up_weight, down_weight)


def on_device(
    points,
    lengths,
    send_blocks,
    pattern,
    ln1_gain,
    qk_weight,
    v_weight,
    o_weight,
    ln2_gain,
    up_weight,
    down_weight,
):
    rows, width = points.shape
    block_rows = rows // pattern.shape[0]
    gain1, gain2 = ln1_gain[None, :], ln2_gain[None, :]
    to_right, to_left = pack(points, send_blocks[0], lengths, block_rows)
    left = passed_along(to_right, "patch", 1)
    right = passed_along(to_left, "patch", -1)
    scale = LOG2E / math.sqrt(width // H)
    queries, keys, values = project(points, gain1, qk_weight, v_weight, scale)
    attended = attend(
        queries, keys, values, left, right, pattern, lengths, gain1, qk_weight, v_weight
    )
    return mix(points, attended, lengths, o_weight, gain2, up_weight, down_weight)


def solution(mesh):
    in_specs = (
        P(("groups", "patch"), None),
        P(("groups", "patch")),
        P(("groups", "patch"), None, None),
        P(("groups", "patch"), None),
        P(),
        P(),
        P(),
        P(),
        P(),
        P(),
        P(),
    )
    out_specs = P(("groups", "patch"), None)
    return jax.shard_map(
        on_device, mesh=mesh, in_specs=in_specs, out_specs=out_specs, check_vma=False
    )
```

```python
import functools
import math

import jax
import jax.numpy as jnp
from jax import lax
from jax.experimental import pallas as pl
from jax.experimental.pallas import tpu as pltpu
from jax.sharding import PartitionSpec as P

H = 32
LANES = 128
MARK = 1000.0
NEG = -1000000000.0
LOG2E = 1.4426950408889634
STACK = 2


def passed_along(array, axis, by):
    count = lax.axis_size(axis)
    pairs = [(i, i + by) for i in range(count) if 0 <= i + by < count]
    return lax.ppermute(array, axis, pairs)


def layer_norm(inputs, gain):
    center = inputs - jnp.mean(inputs, axis=-1, keepdims=True)
    spread = jnp.mean(center * center, axis=-1, keepdims=True)
    return center * lax.rsqrt(spread + 1e-05) * gain


def pack_kernel(send_ref, length_ref, *refs):
    sources, targets = refs[:-2], refs[-2:]
    sides, count = send_ref.shape
    rows = sources[0].shape[0]
    for side in range(sides):
        for slot in range(count):
            source = sources[side * count + slot]
            position = send_ref[side, slot] * rows + lax.broadcasted_iota(
                jnp.int32, source.shape, 0
            )
            value = jnp.where(position < length_ref[0], source[...].astype(jnp.float32), MARK)
            targets[side][slot * rows : (slot + 1) * rows, :] = value.astype(source.dtype)


def pack(points, send, lengths, block_rows):
    width = points.shape[1]
    sides, count = send.shape
    shape = jax.ShapeDtypeStruct((count * block_rows, width), points.dtype)

    def picked(side, slot):
        return pl.BlockSpec((block_rows, width), lambda i, send, _: (send[side, slot], 0))

    return pl.pallas_call(
        pack_kernel,
        out_shape=(shape, shape),
        grid_spec=pltpu.PrefetchScalarGridSpec(
            num_scalar_prefetch=2,
            grid=(1,),
            in_specs=[picked(side, slot) for side in range(sides) for slot in range(count)],
            out_specs=[pl.BlockSpec(shape.shape, lambda i, *_: (0, 0))] * 2,
        ),
        name="pack",
    )(send, lengths, *([points] * (sides * count)))


def project_kernel(scale, x_ref, gain_ref, qk_ref, v_ref, q_out, k_out, v_out):
    normed = layer_norm(x_ref[...].astype(jnp.float32), gain_ref[...]).astype(jnp.bfloat16)
    queries = jnp.dot(normed, qk_ref[0], preferred_element_type=jnp.float32)
    q_out[...] = (queries * scale).astype(q_out.dtype)
    k_out[...] = jnp.dot(normed, qk_ref[1], preferred_element_type=jnp.float32).astype(k_out.dtype)
    v_out[...] = jnp.dot(normed, v_ref[...], preferred_element_type=jnp.float32).astype(v_out.dtype)


def project(points, gain, qk_weight, v_weight, scale, tile=256):
    rows, width = points.shape
    shape = jax.ShapeDtypeStruct((rows, width), jnp.bfloat16)
    row_spec = pl.BlockSpec((tile, width), lambda i: (i, 0))
    return pl.pallas_call(
        functools.partial(project_kernel, scale),
        out_shape=(shape, shape, shape),
        grid=(rows // tile,),
        in_specs=[
            row_spec,
            pl.BlockSpec(gain.shape, lambda i: (0, 0)),
            pl.BlockSpec(qk_weight.shape, lambda i: (0, 0, 0)),
            pl.BlockSpec(v_weight.shape, lambda i: (0, 0)),
        ],
        out_specs=[row_spec] * 3,
        cost_estimate=pl.CostEstimate(
            flops=6 * rows * width * width,
            bytes_accessed=8 * rows * width + 6 * width * width,
            transcendentals=0,
        ),
        compiler_params=pltpu.CompilerParams(vmem_limit_bytes=16 << 20),
        name="project",
    )(points, gain, qk_weight, v_weight)


def attend_kernel(
    block_rows,
    head_size,
    pattern_ref,
    length_ref,
    q_ref,
    k_ref,
    v_ref,
    left_ref,
    right_ref,
    gain_ref,
    wk_ref,
    wv_ref,
    out_ref,
    k_pool,
    v_pool,
    b_pool,
):
    step = pl.program_id(0)
    local, width = k_ref.shape
    offered = left_ref.shape[0]
    per_tile = LANES // head_size
    first_lane = lambda shape: lax.broadcasted_iota(jnp.int32, shape, 1) == 0

    @pl.when(step == 0)
    def _():
        k_pool[0:local, :] = k_ref[...]
        v_pool[0:local, :] = v_ref[...]
        position = lax.broadcasted_iota(jnp.int32, (local, LANES), 0)
        dead = (position >= length_ref[0]) & first_lane((local, LANES))
        b_pool[0:local, :] = jnp.where(dead, NEG, 0.0).astype(b_pool.dtype)
        for index, source in enumerate((left_ref, right_ref)):
            start = local + index * offered
            rows = source[...].astype(jnp.float32)
            normed = layer_norm(rows, gain_ref[...]).astype(jnp.bfloat16)
            k_pool[start : start + offered, :] = jnp.dot(
                normed, wk_ref[0], preferred_element_type=jnp.float32
            ).astype(k_pool.dtype)
            v_pool[start : start + offered, :] = jnp.dot(
                normed, wv_ref[...], preferred_element_type=jnp.float32
            ).astype(v_pool.dtype)
            dead = (rows[:, 0:LANES] > 0.5 * MARK) & first_lane((offered, LANES))
            b_pool[start : start + offered, :] = jnp.where(dead, NEG, 0.0).astype(b_pool.dtype)

    slots = [step] + [pattern_ref[step, s] for s in range(pattern_ref.shape[1])]
    starts = [pl.multiple_of(slot * block_rows, block_rows) for slot in slots]
    lane = lax.broadcasted_iota(jnp.int32, (block_rows, LANES), 1)
    unit = jnp.where(lane == 0, 1.0, 0.0).astype(jnp.bfloat16)
    bias = jnp.concatenate([b_pool[pl.ds(start, block_rows), :] for start in starts], axis=0)
    ones = jnp.ones((len(slots) * block_rows, LANES), jnp.bfloat16)

    for tile in range(width // LANES):
        columns = pl.ds(tile * LANES, LANES)
        keys = jnp.concatenate(
            [k_pool[pl.ds(start, block_rows), columns] for start in starts], axis=0
        )
        values = jnp.concatenate(
            [v_pool[pl.ds(start, block_rows), columns] for start in starts], axis=0
        )
        keys = jnp.concatenate([keys, bias], axis=1)
        values = jnp.concatenate([values, ones], axis=1)
        queries = q_ref[:, columns].astype(jnp.float32)
        top = bottom = None
        for group in range(0, per_tile, STACK):
            heads = range(group, group + STACK)
            stacked = jnp.concatenate(
                [
                    jnp.concatenate(
                        [
                            jnp.where(lane // head_size == head, queries, 0.0).astype(jnp.bfloat16),
                            unit,
                        ],
                        axis=1,
                    )
                    for head in heads
                ],
                axis=0,
            )
            scores = lax.dot_general(
                stacked, keys, (((1,), (1,)), ((), ())), preferred_element_type=jnp.float32
            )
            expo = jnp.exp2(scores - jnp.max(scores, axis=-1, keepdims=True)).astype(jnp.bfloat16)
            mixed = jnp.dot(expo, values, preferred_element_type=jnp.float32)
            for index, head in enumerate(heads):
                part = mixed[index * block_rows : (index + 1) * block_rows]
                num, den = part[:, :LANES], part[:, LANES:]
                if top is None:
                    top, bottom = num, den
                else:
                    mine = lane // head_size == head
                    top = jnp.where(mine, num, top)
                    bottom = jnp.where(mine, den, bottom)
        out_ref[:, columns] = (top / bottom).astype(out_ref.dtype)


def attend(queries, keys, values, left, right, pattern, lengths, gain, qk_weight, v_weight):
    rows, width = queries.shape
    blocks = pattern.shape[0]
    block_rows = rows // blocks
    pool = rows + left.shape[0] + right.shape[0]
    row_spec = pl.BlockSpec((block_rows, width), lambda i, *_: (i, 0))
    whole = lambda shape: pl.BlockSpec(shape, lambda i, *_: (0,) * len(shape))
    return pl.pallas_call(
        functools.partial(attend_kernel, block_rows, width // H),
        out_shape=jax.ShapeDtypeStruct((rows, width), jnp.bfloat16),
        grid_spec=pltpu.PrefetchScalarGridSpec(
            num_scalar_prefetch=2,
            grid=(blocks,),
            in_specs=[
                row_spec,
                whole(keys.shape),
                whole(values.shape),
                whole(left.shape),
                whole(right.shape),
                whole(gain.shape),
                pl.BlockSpec((1, width, width), lambda i, *_: (1, 0, 0)),
                whole(v_weight.shape),
            ],
            out_specs=row_spec,
            scratch_shapes=[
                pltpu.VMEM((pool, width), jnp.bfloat16),
                pltpu.VMEM((pool, width), jnp.bfloat16),
                pltpu.VMEM((pool, LANES), jnp.bfloat16),
            ],
        ),
        compiler_params=pltpu.CompilerParams(vmem_limit_bytes=24 << 20),
        name="attend",
    )(pattern, lengths, queries, keys, values, left, right, gain, qk_weight, v_weight)


def mix_kernel(length_ref, x_ref, a_ref, wo_ref, gain_ref, up_ref, down_ref, out_ref):
    rows = x_ref.shape[0]
    mixed = x_ref[...].astype(jnp.float32) + jnp.dot(
        a_ref[...], wo_ref[...], preferred_element_type=jnp.float32
    )
    normed = layer_norm(mixed, gain_ref[...]).astype(jnp.bfloat16)
    inner = jnp.dot(normed, up_ref[...], preferred_element_type=jnp.float32)
    hidden = (0.5 * inner * (1.0 + lax.erf(inner * math.sqrt(0.5)))).astype(jnp.bfloat16)
    result = mixed + jnp.dot(hidden, down_ref[...], preferred_element_type=jnp.float32)
    position = pl.program_id(0) * rows + lax.broadcasted_iota(jnp.int32, result.shape, 0)
    out_ref[...] = jnp.where(position < length_ref[0], result, 0.0).astype(out_ref.dtype)


def mix(points, attended, lengths, o_weight, gain, up_weight, down_weight, tile=256):
    rows, width = points.shape
    row_spec = pl.BlockSpec((tile, width), lambda i, *_: (i, 0))
    whole = lambda shape: pl.BlockSpec(shape, lambda i, *_: (0,) * len(shape))
    return pl.pallas_call(
        mix_kernel,
        out_shape=jax.ShapeDtypeStruct((rows, width), jnp.bfloat16),
        grid_spec=pltpu.PrefetchScalarGridSpec(
            num_scalar_prefetch=1,
            grid=(rows // tile,),
            in_specs=[
                row_spec,
                row_spec,
                whole(o_weight.shape),
                whole(gain.shape),
                whole(up_weight.shape),
                whole(down_weight.shape),
            ],
            out_specs=row_spec,
        ),
        compiler_params=pltpu.CompilerParams(vmem_limit_bytes=24 << 20),
        name="mix",
    )(lengths, points, attended, o_weight, gain, up_weight, down_weight)


def on_device(
    points,
    lengths,
    send_blocks,
    pattern,
    ln1_gain,
    qk_weight,
    v_weight,
    o_weight,
    ln2_gain,
    up_weight,
    down_weight,
):
    rows, width = points.shape
    block_rows = rows // pattern.shape[0]
    gain1, gain2 = ln1_gain[None, :], ln2_gain[None, :]
    to_left, to_right = pack(points, send_blocks[0], lengths, block_rows)
    left = passed_along(to_right, "patch", 1)
    right = passed_along(to_left, "patch", -1)
    scale = LOG2E / math.sqrt(width // H)
    queries, keys, values = project(points, gain1, qk_weight, v_weight, scale)
    attended = attend(
        queries, keys, values, left, right, pattern, lengths, gain1, qk_weight, v_weight
    )
    return mix(points, attended, lengths, o_weight, gain2, up_weight, down_weight)


def solution(mesh):
    in_specs = (
        P(("groups", "patch"), None),
        P(("groups", "patch")),
        P(("groups", "patch"), None, None),
        P(("groups", "patch"), None),
        P(),
        P(),
        P(),
        P(),
        P(),
        P(),
        P(),
    )
    out_specs = P(("groups", "patch"), None)
    return jax.shard_map(
        on_device, mesh=mesh, in_specs=in_specs, out_specs=out_specs, check_vma=False
    )
```

```python
import functools
import math

import jax
import jax.numpy as jnp
from jax import lax
from jax.experimental import pallas as pl
from jax.experimental.pallas import tpu as pltpu
from jax.sharding import PartitionSpec as P

H = 32
LANES = 128
MARK = 1000.0
NEG = -1000000000.0
LOG2E = 1.4426950408889634
STACK = 2


def passed_along(array, axis, by):
    count = lax.axis_size(axis)
    pairs = [(i, i + by) for i in range(count) if 0 <= i + by < count]
    return lax.ppermute(array, axis, pairs)


def layer_norm(inputs, gain):
    center = inputs - jnp.mean(inputs, axis=-1, keepdims=True)
    spread = jnp.mean(center * center, axis=-1, keepdims=True)
    return center * lax.rsqrt(spread + 1e-05) * gain


def pack_kernel(send_ref, length_ref, *refs):
    sources, targets = refs[:-2], refs[-2:]
    sides, count = send_ref.shape
    rows = sources[0].shape[0]
    for side in range(sides):
        for slot in range(count):
            source = sources[side * count + slot]
            position = send_ref[side, slot] * rows + lax.broadcasted_iota(
                jnp.int32, source.shape, 0
            )
            value = jnp.where(position < length_ref[0], source[...].astype(jnp.float32), MARK)
            targets[side][slot * rows : (slot + 1) * rows, :] = value.astype(source.dtype)


def pack(points, send, lengths, block_rows):
    width = points.shape[1]
    sides, count = send.shape
    shape = jax.ShapeDtypeStruct((count * block_rows, width), points.dtype)

    def picked(side, slot):
        return pl.BlockSpec((block_rows, width), lambda i, send, _: (send[side, slot], 0))

    return pl.pallas_call(
        pack_kernel,
        out_shape=(shape, shape),
        grid_spec=pltpu.PrefetchScalarGridSpec(
            num_scalar_prefetch=2,
            grid=(1,),
            in_specs=[picked(side, slot) for side in range(sides) for slot in range(count)],
            out_specs=[pl.BlockSpec(shape.shape, lambda i, *_: (0, 0))] * 2,
        ),
        name="pack",
    )(send, lengths, *([points] * (sides * count)))


def project_kernel(scale, x_ref, gain_ref, qk_ref, v_ref, q_out, k_out, v_out):
    normed = layer_norm(x_ref[...].astype(jnp.float32), gain_ref[...]).astype(jnp.bfloat16)
    queries = jnp.dot(normed, qk_ref[0], preferred_element_type=jnp.float32)
    q_out[...] = (queries * scale).astype(q_out.dtype)
    k_out[...] = jnp.dot(normed, qk_ref[1], preferred_element_type=jnp.float32).astype(k_out.dtype)
    v_out[...] = jnp.dot(normed, v_ref[...], preferred_element_type=jnp.float32).astype(v_out.dtype)


def project(points, gain, qk_weight, v_weight, scale, tile=512):
    rows, width = points.shape
    shape = jax.ShapeDtypeStruct((rows, width), jnp.bfloat16)
    row_spec = pl.BlockSpec((tile, width), lambda i: (i, 0))
    return pl.pallas_call(
        functools.partial(project_kernel, scale),
        out_shape=(shape, shape, shape),
        grid=(rows // tile,),
        in_specs=[
            row_spec,
            pl.BlockSpec(gain.shape, lambda i: (0, 0)),
            pl.BlockSpec(qk_weight.shape, lambda i: (0, 0, 0)),
            pl.BlockSpec(v_weight.shape, lambda i: (0, 0)),
        ],
        out_specs=[row_spec] * 3,
        cost_estimate=pl.CostEstimate(
            flops=6 * rows * width * width,
            bytes_accessed=8 * rows * width + 6 * width * width,
            transcendentals=0,
        ),
        compiler_params=pltpu.CompilerParams(vmem_limit_bytes=16 << 20),
        name="project",
    )(points, gain, qk_weight, v_weight)


def attend_kernel(
    block_rows,
    head_size,
    pattern_ref,
    length_ref,
    q_ref,
    k_ref,
    v_ref,
    left_ref,
    right_ref,
    gain_ref,
    wk_ref,
    wv_ref,
    out_ref,
    k_pool,
    v_pool,
    b_pool,
):
    step = pl.program_id(0)
    local, width = k_ref.shape
    offered = left_ref.shape[0]
    per_tile = LANES // head_size
    first_lane = lambda shape: lax.broadcasted_iota(jnp.int32, shape, 1) == 0

    @pl.when(step == 0)
    def _():
        k_pool[0:local, :] = k_ref[...]
        v_pool[0:local, :] = v_ref[...]
        position = lax.broadcasted_iota(jnp.int32, (local, LANES), 0)
        dead = (position >= length_ref[0]) & first_lane((local, LANES))
        b_pool[0:local, :] = jnp.where(dead, NEG, 0.0).astype(b_pool.dtype)
        for index, source in enumerate((left_ref, right_ref)):
            start = local + index * offered
            rows = source[...].astype(jnp.float32)
            normed = layer_norm(rows, gain_ref[...]).astype(jnp.bfloat16)
            k_pool[start : start + offered, :] = jnp.dot(
                normed, wk_ref[0], preferred_element_type=jnp.float32
            ).astype(k_pool.dtype)
            v_pool[start : start + offered, :] = jnp.dot(
                normed, wv_ref[...], preferred_element_type=jnp.float32
            ).astype(v_pool.dtype)
            dead = (rows[:, 0:LANES] > 0.5 * MARK) & first_lane((offered, LANES))
            b_pool[start : start + offered, :] = jnp.where(dead, NEG, 0.0).astype(b_pool.dtype)

    slots = [step] + [pattern_ref[step, s] for s in range(pattern_ref.shape[1])]
    starts = [pl.multiple_of(slot * block_rows, block_rows) for slot in slots]
    lane = lax.broadcasted_iota(jnp.int32, (block_rows, LANES), 1)
    unit = jnp.where(lane == 0, 1.0, 0.0).astype(jnp.bfloat16)
    bias = jnp.concatenate([b_pool[pl.ds(start, block_rows), :] for start in starts], axis=0)
    ones = jnp.ones((len(slots) * block_rows, LANES), jnp.bfloat16)

    for tile in range(width // LANES):
        columns = pl.ds(tile * LANES, LANES)
        keys = jnp.concatenate(
            [k_pool[pl.ds(start, block_rows), columns] for start in starts], axis=0
        )
        values = jnp.concatenate(
            [v_pool[pl.ds(start, block_rows), columns] for start in starts], axis=0
        )
        keys = jnp.concatenate([keys, bias], axis=1)
        values = jnp.concatenate([values, ones], axis=1)
        queries = q_ref[:, columns].astype(jnp.float32)
        top = bottom = None
        for group in range(0, per_tile, STACK):
            heads = range(group, group + STACK)
            stacked = jnp.concatenate(
                [
                    jnp.concatenate(
                        [
                            jnp.where(lane // head_size == head, queries, 0.0).astype(jnp.bfloat16),
                            unit,
                        ],
                        axis=1,
                    )
                    for head in heads
                ],
                axis=0,
            )
            scores = lax.dot_general(
                stacked, keys, (((1,), (1,)), ((), ())), preferred_element_type=jnp.float32
            )
            expo = jnp.exp2(scores - jnp.max(scores, axis=-1, keepdims=True)).astype(jnp.bfloat16)
            mixed = jnp.dot(expo, values, preferred_element_type=jnp.float32)
            for index, head in enumerate(heads):
                part = mixed[index * block_rows : (index + 1) * block_rows]
                num, den = part[:, :LANES], part[:, LANES:]
                if top is None:
                    top, bottom = num, den
                else:
                    mine = lane // head_size == head
                    top = jnp.where(mine, num, top)
                    bottom = jnp.where(mine, den, bottom)
        out_ref[:, columns] = (top / bottom).astype(out_ref.dtype)


def attend(queries, keys, values, left, right, pattern, lengths, gain, qk_weight, v_weight):
    rows, width = queries.shape
    blocks = pattern.shape[0]
    block_rows = rows // blocks
    pool = rows + left.shape[0] + right.shape[0]
    row_spec = pl.BlockSpec((block_rows, width), lambda i, *_: (i, 0))
    whole = lambda shape: pl.BlockSpec(shape, lambda i, *_: (0,) * len(shape))
    return pl.pallas_call(
        functools.partial(attend_kernel, block_rows, width // H),
        out_shape=jax.ShapeDtypeStruct((rows, width), jnp.bfloat16),
        grid_spec=pltpu.PrefetchScalarGridSpec(
            num_scalar_prefetch=2,
            grid=(blocks,),
            in_specs=[
                row_spec,
                whole(keys.shape),
                whole(values.shape),
                whole(left.shape),
                whole(right.shape),
                whole(gain.shape),
                pl.BlockSpec((1, width, width), lambda i, *_: (1, 0, 0)),
                whole(v_weight.shape),
            ],
            out_specs=row_spec,
            scratch_shapes=[
                pltpu.VMEM((pool, width), jnp.bfloat16),
                pltpu.VMEM((pool, width), jnp.bfloat16),
                pltpu.VMEM((pool, LANES), jnp.bfloat16),
            ],
        ),
        compiler_params=pltpu.CompilerParams(vmem_limit_bytes=24 << 20),
        name="attend",
    )(pattern, lengths, queries, keys, values, left, right, gain, qk_weight, v_weight)


def mix_kernel(length_ref, x_ref, a_ref, wo_ref, gain_ref, up_ref, down_ref, out_ref):
    rows = x_ref.shape[0]
    mixed = x_ref[...].astype(jnp.float32) + jnp.dot(
        a_ref[...], wo_ref[...], preferred_element_type=jnp.float32
    )
    normed = layer_norm(mixed, gain_ref[...]).astype(jnp.bfloat16)
    inner = jnp.dot(normed, up_ref[...], preferred_element_type=jnp.float32)
    hidden = (0.5 * inner * (1.0 + lax.erf(inner * math.sqrt(0.5)))).astype(jnp.bfloat16)
    result = mixed + jnp.dot(hidden, down_ref[...], preferred_element_type=jnp.float32)
    position = pl.program_id(0) * rows + lax.broadcasted_iota(jnp.int32, result.shape, 0)
    out_ref[...] = jnp.where(position < length_ref[0], result, 0.0).astype(out_ref.dtype)


def mix(points, attended, lengths, o_weight, gain, up_weight, down_weight, tile=512):
    rows, width = points.shape
    row_spec = pl.BlockSpec((tile, width), lambda i, *_: (i, 0))
    whole = lambda shape: pl.BlockSpec(shape, lambda i, *_: (0,) * len(shape))
    return pl.pallas_call(
        mix_kernel,
        out_shape=jax.ShapeDtypeStruct((rows, width), jnp.bfloat16),
        grid_spec=pltpu.PrefetchScalarGridSpec(
            num_scalar_prefetch=1,
            grid=(rows // tile,),
            in_specs=[
                row_spec,
                row_spec,
                whole(o_weight.shape),
                whole(gain.shape),
                whole(up_weight.shape),
                whole(down_weight.shape),
            ],
            out_specs=row_spec,
        ),
        compiler_params=pltpu.CompilerParams(vmem_limit_bytes=24 << 20),
        name="mix",
    )(lengths, points, attended, o_weight, gain, up_weight, down_weight)


def on_device(
    points,
    lengths,
    send_blocks,
    pattern,
    ln1_gain,
    qk_weight,
    v_weight,
    o_weight,
    ln2_gain,
    up_weight,
    down_weight,
):
    rows, width = points.shape
    block_rows = rows // pattern.shape[0]
    gain1, gain2 = ln1_gain[None, :], ln2_gain[None, :]
    to_left, to_right = pack(points, send_blocks[0], lengths, block_rows)
    left = passed_along(to_right, "patch", 1)
    right = passed_along(to_left, "patch", -1)
    scale = LOG2E / math.sqrt(width // H)
    queries, keys, values = project(points, gain1, qk_weight, v_weight, scale)
    attended = attend(
        queries, keys, values, left, right, pattern, lengths, gain1, qk_weight, v_weight
    )
    return mix(points, attended, lengths, o_weight, gain2, up_weight, down_weight)


def solution(mesh):
    in_specs = (
        P(("groups", "patch"), None),
        P(("groups", "patch")),
        P(("groups", "patch"), None, None),
        P(("groups", "patch"), None),
        P(),
        P(),
        P(),
        P(),
        P(),
        P(),
        P(),
    )
    out_specs = P(("groups", "patch"), None)
    return jax.shard_map(
        on_device, mesh=mesh, in_specs=in_specs, out_specs=out_specs, check_vma=False
    )
```
